1024 devices in a mesh: dp: 16 (over z), shard: 64 (over y, x, core).
Axes of the slice: x: 4, y: 8, z: 16, core: 2. Of those that a mesh axis runs over, the one named last changes fastest.
Arguments:
- partials: bfloat16 [16, 2, 1024, 8192], P('dp', None, 'shard'), may hold values from -6 to 6
- block_owner: int32 [64], replicated, may hold values from 0 to 63, as said below
- owner_slot: int32 [64], replicated, may hold values from 0 to 0, as said below
- fac_left: float32 [64, 512, 512], P('shard'), may hold values from -6 to 6
- fac_right: float32 [64, 512, 512], P('shard'), may hold values from -6 to 6
- moment: bfloat16 [64, 512, 512], P('shard'), may hold values from -12 to 12
- second: float32 [64, 512, 512], P('shard'), may hold values from 1 to 16
- basis_left: bfloat16 [64, 512, 512], P('shard'), may hold values from -1 to 1, as said below
- basis_right: bfloat16 [64, 512, 512], P('shard'), may hold values from -1 to 1, as said below
Outputs:
- update: bfloat16 [2, 1024, 8192], P(None, 'shard')
- fac_left_new: float32 [64, 512, 512], P('shard')
- fac_right_new: float32 [64, 512, 512], P('shard')
- moment_new: bfloat16 [64, 512, 512], P('shard')
- second_new: float32 [64, 512, 512], P('shard')
The draws below stay inside these ranges and needn't reach their ends.
Inputs may be any that keep to these rules, and one draw needn't show every extreme that they name: `block_owner`: each owner is named by exactly 1 block. `owner_slot`: the blocks of one owner have distinct slots. `basis_left`: each block is an orthogonal matrix rounded to bfloat16. `basis_right`: each block is an orthogonal matrix rounded to bfloat16.
All inputs are finite; a program needn't handle non-finite values.
Results may differ from the reference program's by a relative error of at most 0.018.
Values may be sent and summed in bfloat16 or wider, within the bound.
A program may use at most 32 MiB of HBM per device.

```python
import math
import jax
import jax.numpy as jnp
from jax import lax

ORDER = 8192
BLK = 512
BROW = 2
CB = 16
NB = 64
BPD = 1
BAND = 1024
N_DP = 16


def placement_order(key):
    return jax.random.permutation(jax.random.fold_in(key, 11), NB)


def draw_block_owner(key, part):
    return (placement_order(key) // BPD).astype(jnp.int32)


def draw_owner_slot(key, part):
    return (placement_order(key) % BPD).astype(jnp.int32)


def orthogonal_blocks(key, salt):
    normal_draw = jax.random.normal(jax.random.fold_in(key, salt), (NB, BLK, BLK), jnp.float32)
    factor_q, factor_r = jnp.linalg.qr(normal_draw)
    return factor_q.astype(jnp.bfloat16)


def draw_basis_left(key, part):
    return orthogonal_blocks(key, 23)


def draw_basis_right(key, part):
    return orthogonal_blocks(key, 37)


def block_levels(key, dims, shards, smallest, high):
    def one(dim, blocks):
        steps = jax.random.uniform(jax.random.fold_in(jax.random.fold_in(key, 6), dim), (blocks,), jnp.float32, smallest / len(shards), high / len(shards))
        return jnp.repeat(jnp.exp(steps), dims[dim] // blocks).reshape((-1,) + (1,) * (len(dims) - dim - 1))

    level = one(*shards[0])
    for cut in shards[1:]:
        level = level * one(*cut)
    return level


def bell_draw(own_key, extent, width, limit, pieces=(), dtype=jnp.bfloat16):
    values = width * jax.random.normal(own_key, extent, jnp.float32)
    if pieces:
        values = values * block_levels(own_key, extent, pieces, -0.22, 0.18)
    return jnp.clip(values, -limit, limit).astype(dtype)


def setup_inputs(seed: int = 0) -> dict:
    streams_of = jax.random.split(jax.random.key(seed), 10)
    partials = bell_draw(streams_of[0], (N_DP, 2, BAND, ORDER), 1.0, 6.0, ((0, 16), (2, 64)))
    block_owner = draw_block_owner(jax.random.fold_in(streams_of[9], 71), 0)
    owner_slot = draw_owner_slot(jax.random.fold_in(streams_of[9], 71), 0)
    fac_left = bell_draw(streams_of[3], (NB, BLK, BLK), 1.0, 6.0, ((0, 64),), jnp.float32)
    fac_right = bell_draw(streams_of[4], (NB, BLK, BLK), 1.0, 6.0, ((0, 64),), jnp.float32)
    moment = bell_draw(streams_of[5], (NB, BLK, BLK), 2.0, 12.0, ((0, 64),))
    second = jnp.clip(jnp.exp(math.log(16.0) - 2.7725887 * jax.random.uniform(streams_of[6], (NB, BLK, BLK), jnp.float32) ** block_levels(streams_of[6], (NB, BLK, BLK), ((0, 64),), -0.2, 0.2)), 1.0, 16.0)
    basis_left = draw_basis_left(jax.random.fold_in(streams_of[9], 71), 0)
    basis_right = draw_basis_right(jax.random.fold_in(streams_of[9], 71), 0)
    return {"partials": partials, "block_owner": block_owner, "owner_slot": owner_slot, "fac_left": fac_left, "fac_right": fac_right, "moment": moment, "second": second, "basis_left": basis_left, "basis_right": basis_right}


def block_views(grad_band):
    divided = grad_band.reshape(2, BROW, BLK, CB, BLK)
    return jnp.transpose(divided, (0, 1, 3, 2, 4)).reshape(NB, BLK, BLK)

def rotate_into(matrix, basis_one, basis_two):
    rotated_half = jnp.dot(basis_one.T.astype(jnp.float32), matrix.astype(jnp.float32), preferred_element_type=jnp.float32).astype(jnp.bfloat16)
    return jnp.dot(rotated_half.astype(jnp.float32), basis_two.astype(jnp.float32), preferred_element_type=jnp.float32)

def update_block(inputs):
    grads, left_old, right_old, moment_old, second_old, basis_one, basis_two = inputs
    left_new = 0.95 * left_old + 0.05 * jnp.dot(grads.astype(jnp.float32), grads.T.astype(jnp.float32), preferred_element_type=jnp.float32)
    right_new = 0.95 * right_old + 0.05 * jnp.dot(grads.T.astype(jnp.float32), grads.astype(jnp.float32), preferred_element_type=jnp.float32)
    moment_next = (0.9 * moment_old.astype(jnp.float32) + 0.1 * grads.astype(jnp.float32)).astype(jnp.bfloat16)
    grad_rotated = rotate_into(grads, basis_one, basis_two)
    second_next = 0.95 * second_old + 0.05 * grad_rotated * grad_rotated
    moment_rotated = rotate_into(moment_next, basis_one, basis_two)
    scaled = (moment_rotated / (jnp.sqrt(second_next) + 1e-08)).astype(jnp.bfloat16)
    back_half = jnp.dot(basis_one.astype(jnp.float32), scaled.astype(jnp.float32), preferred_element_type=jnp.float32).astype(jnp.bfloat16)
    update_one = jnp.dot(back_half.astype(jnp.float32), basis_two.T.astype(jnp.float32), preferred_element_type=jnp.float32).astype(jnp.bfloat16)
    return (left_new, right_new, moment_next, second_next, update_one)

def reference(partials, block_owner, owner_slot, fac_left, fac_right, moment, second, basis_left, basis_right):
    grad = lax.optimization_barrier(jnp.sum(partials.astype(jnp.float32), axis=0)).astype(jnp.bfloat16)
    position = (block_owner * BPD + owner_slot).astype(jnp.int32)
    numbering = jnp.arange(NB).astype(jnp.int32)
    matches = position[:, None] == numbering[None, :]
    block_at = lax.optimization_barrier(jnp.sum(jnp.where(matches, numbering[:, None], 0), axis=0)).astype(jnp.int32)
    grad_blocks = block_views(grad)[block_at]
    results = lax.map(update_block, (grad_blocks, fac_left, fac_right, moment, second, basis_left, basis_right))
    left_new, right_new, moment_next, second_next, update_blocks = results
    by_block = update_blocks[position]
    update = jnp.transpose(by_block.reshape(2, BROW, CB, BLK, BLK), (0, 1, 3, 2, 4)).reshape(2, BAND, ORDER)
    return (update, left_new, right_new, moment_next, second_next)
```

```python
import functools

import jax
import jax.numpy as jnp
from jax import lax
from jax.experimental import pallas as pl
from jax.experimental.pallas import tpu as pltpu
from jax.sharding import PartitionSpec as P

MESH = pl.DeviceIdType.MESH
F32 = jnp.float32
BF16 = jnp.bfloat16
VMEM_LIMIT = 60 << 20


def dot(a, b):
    return jnp.dot(a, b, preferred_element_type=F32)


def dot_tn(a, b):
    return lax.dot_general(a, b, (((0,), (0,)), ((), ())), preferred_element_type=F32)


def dot_nt(a, b):
    return lax.dot_general(a, b, (((1,), (1,)), ((), ())), preferred_element_type=F32)


class Place:
    def __init__(self, nz, ny, nx):
        self.nz, self.ny, self.nx = nz, ny, nx
        self.z = lax.axis_index("dp")
        self.s = lax.axis_index("shard")
        self.y = self.s // nx
        self.xc = self.s % nx

    def at_z(self, step):
        return ((self.z + self.nz + step) % self.nz, self.s)

    def at_xc(self, xc):
        return (self.z, self.y * self.nx + xc)

    def at_y(self, y):
        return (self.z, y * self.nx + self.xc)

    def slot(self, step):
        return (self.z + 2 * self.nz + step) % self.nz


def enter(at):
    barrier = pltpu.get_barrier_semaphore()

    def signal(peer):
        pl.semaphore_signal(barrier, inc=1, device_id=peer, device_id_type=MESH)

    steps = sorted({abs(child - parent) for parent, child in TREE})
    for step in steps:
        signal(at.at_z(step))
        signal(at.at_z(-step))

    def to_xc(step, carry):
        signal(at.at_xc((at.xc + step) % at.nx))
        return carry

    def to_y(step, carry):
        signal(at.at_y((at.y + step) % at.ny))
        return carry

    lax.fori_loop(1, at.nx, to_xc, 0)
    lax.fori_loop(1, at.ny, to_y, 0)
    pl.semaphore_wait(barrier, 2 * len(steps) + at.nx - 1 + at.ny - 1)


def remote(src, dst, send_sem, recv_sem, peer):
    return pltpu.make_async_remote_copy(
        src_ref=src,
        dst_ref=dst,
        send_sem=send_sem,
        recv_sem=recv_sem,
        device_id=peer,
        device_id_type=MESH,
    )


def swap(count, mine, peer_of, out_buf, in_buf, send_sem, recv_sem, meanwhile=None):
    def start(step, carry):
        j = (mine + step) % count
        remote(out_buf.at[j], in_buf.at[mine], send_sem.at[j], recv_sem.at[mine], peer_of(j)).start()
        return carry

    def finish(step, carry):
        j = (mine + step) % count
        remote(out_buf.at[j], in_buf.at[j], send_sem.at[j], recv_sem.at[j], peer_of(j)).wait_recv()
        return carry

    def drain(step, carry):
        j = (mine + step) % count
        remote(out_buf.at[j], in_buf.at[j], send_sem.at[j], recv_sem.at[j], peer_of(j)).wait_send()
        return carry

    lax.fori_loop(1, count, start, 0)
    in_buf[mine] = out_buf[mine]
    if meanwhile is not None:
        meanwhile()
    lax.fori_loop(1, count, finish, 0)
    return lambda: lax.fori_loop(1, count, drain, 0)


def rows_of(buf, count):
    return jnp.concatenate([buf[j].astype(F32) for j in range(count)], axis=0)


def put_rows(buf, rows, count):
    height = rows.shape[0] // count
    for j in range(count):
        buf[j] = rows[j * height : (j + 1) * height].astype(BF16)


def turned(rows, outer, inner):
    total = outer * inner
    row = lax.broadcasted_iota(jnp.int32, (total, total), 0)
    col = lax.broadcasted_iota(jnp.int32, (total, total), 1)
    pick = (col == (row % outer) * inner + row // outer).astype(F32).astype(BF16)
    return dot(pick, rows.astype(BF16))


def mirrored(right, left):
    edges = []
    for k in range(max(len(right), len(left))):
        edges += right[k : k + 1] + [(-a, -b) for a, b in left[k : k + 1]]
    return tuple(edges)


REACH = [(0, 3), (0, 1), (3, 6), (1, 2), (3, 4), (6, 7), (4, 5)]
TREE = mirrored(REACH + [(7, 8)], REACH)


def children(tree, node):
    return [child for parent, child in tree if parent == node]


def spread(at, tree, buf, send_sem, recv_sem):
    parts = buf.shape[1]

    def edge(parent, child, origin, part):
        ref = buf.at[origin, part]
        sems = send_sem.at[child % at.nz, part], recv_sem.at[child % at.nz, part]
        return remote(ref, ref, *sems, at.at_z(child - parent))

    for part in range(parts):
        for child in children(tree, 0):
            edge(0, child, at.z, part).start()
    for parent, node in tree:
        for part in range(parts):
            edge(parent, node, at.slot(-node), part).wait_recv()
            for child in children(tree, node):
                edge(node, child, at.slot(-node), part).start()
    for parent, child in tree:
        for part in range(parts):
            edge(parent, child, at.slot(-parent), part).wait_send()


def collect(at, tree, x, sums, in_buf, send_sem, recv_sem):
    parts = x.shape[0]

    def edge(parent, child, part):
        inner = children(tree, child)
        src = sums.at[child % at.nz, part] if inner else x.at[part, at.slot(-child)]
        sems = send_sem.at[child % at.nz, part], recv_sem.at[child % at.nz, part]
        return remote(src, in_buf.at[child % at.nz, part], *sems, at.at_z(parent - child))

    def total(node, part):
        value = x[part, at.slot(-node)].astype(F32)
        for child in children(tree, node):
            edge(node, child, part).wait_recv()
            value += in_buf[child % at.nz, part].astype(F32)
        return value

    for parent, child in tree[::-1]:
        if not children(tree, child):
            for part in range(parts):
                edge(parent, child, part).start()
    for parent, child in tree[::-1]:
        if children(tree, child):
            for part in range(parts):
                sums[child % at.nz, part] = total(child, part).astype(BF16)
                edge(parent, child, part).start()

    def drain():
        for parent, child in tree:
            for part in range(parts):
                edge(parent, child, part).wait_send()

    return [total(0, part) for part in range(parts)], drain


def to_owners(at, owner, slot, per_owner):
    count = owner.shape[1]
    shape = (at.nx * at.ny, count)
    row = lax.broadcasted_iota(jnp.int32, shape, 0)
    place = (row % at.ny) * at.nx + row // at.ny
    position = owner[...] * per_owner + slot[...]
    return (place == jnp.broadcast_to(position, shape)).astype(F32).astype(BF16)


def step_kernel(sizes, owner, slot, x_in, *refs):
    fl_in, fr_in, moment_in, second_in, bl_in, br_in = refs[:6]
    out, fl_out, fr_out, moment_out, second_out = refs[6:11]
    x, fl, fr, moment, second, bl, br = loaded = refs[11:18]
    sums, in_sums, held, fl_new, fr_new, moment_new, second_new = refs[18:25]
    out_x, in_x, out_y, in_y, back_x, got_x, back_y, got_y = refs[25:33]
    rs_send, rs_recv, ag_send, ag_recv, last_send, last_recv = refs[33:39]
    x_send, x_recv, y_send, y_recv, bx_send, bx_recv, by_send, by_recv = refs[39:47]
    load_sem, store_sem = refs[47:]
    at = Place(*sizes)
    nz, ny, nx = sizes
    size = bl.shape[-1]
    per_z = size // nz
    half = ny // 2
    cb = out.shape[2]

    stored = (x_in, fl_in, fr_in, moment_in, second_in, bl_in, br_in)
    loads = [
        pltpu.make_async_copy(src, dst, load_sem.at[i])
        for i, (src, dst) in enumerate(zip(stored, loaded))
    ]
    for load in loads:
        load.start()
    enter(at)
    loads[0].wait()
    total, z_drain = collect(at, TREE, x, sums, in_sums, rs_send, rs_recv)

    first_band = at.y < half
    pick = to_owners(at, owner, slot, fl.shape[0])
    none = jnp.zeros_like(total[0])
    placed = []
    for m in range(2):
        placed += [jnp.where(first_band, total[m], none), jnp.where(first_band, none, total[m])]
    put_rows(out_x, dot(pick, jnp.concatenate(placed, axis=0).astype(BF16)), nx)
    x_drain = swap(nx, at.xc, at.at_xc, out_x, in_x, x_send, x_recv)
    put_rows(out_y, turned(rows_of(in_x, nx), nx, ny), ny)
    y_drain = swap(ny, at.y, at.at_y, out_y, in_y, y_send, y_recv)
    mine = [in_y[q].astype(F32) + in_y[q + half].astype(F32) for q in range(half)]
    put_rows(held.at[at.z], jnp.concatenate(mine, axis=0), 2)
    spread(at, TREE, held, ag_send, ag_recv)

    row = lax.broadcasted_iota(jnp.int32, (size, size), 0)
    col = lax.broadcasted_iota(jnp.int32, (size, size), 1)
    order = (col == (row % nz) * per_z + row // nz).astype(F32).astype(BF16)
    g = dot(order, held[...].reshape(size, size)).astype(BF16)
    for load in loads[1:]:
        load.wait()
    left, right = bl[0], br[0]
    rotated = dot(dot_tn(left, g).astype(BF16), right)
    second_next = 0.95 * second[0] + 0.05 * rotated * rotated
    second_new[0] = second_next
    moment_next = (0.9 * moment[0].astype(F32) + 0.1 * g.astype(F32)).astype(BF16)
    moment_new[0] = moment_next
    moment_rotated = dot(dot_tn(left, moment_next).astype(BF16), right)
    scaled = (moment_rotated / (jnp.sqrt(second_next) + 1e-8)).astype(BF16)
    mine = lax.broadcasted_iota(jnp.int32, (per_z, size), 0) * nz + at.z
    rows = (lax.broadcasted_iota(jnp.int32, (per_z, size), 1) == mine).astype(F32).astype(BF16)
    back = dot(dot(rows, left).astype(BF16), scaled).astype(BF16)
    update_rows = dot_nt(back, right)

    stores = [
        pltpu.make_async_copy(src, dst, store_sem.at[i])
        for i, (src, dst) in enumerate(
            (
                (second_new, second_out),
                (moment_new, moment_out),
                (fl_new, fl_out),
                (fr_new, fr_out),
            )
        )
    ]

    def left_factor():
        fl_new[0] = 0.95 * fl[0] + 0.05 * dot_nt(g, g)
        for store in stores[:3]:
            store.start()

    def right_factor():
        fr_new[0] = 0.95 * fr[0] + 0.05 * dot_tn(g, g)
        stores[3].start()

    put_rows(back_y, jnp.concatenate([update_rows, update_rows], axis=0), ny)
    by_drain = swap(ny, at.y, at.at_y, back_y, got_y, by_send, by_recv, left_factor)
    put_rows(back_x, turned(rows_of(got_y, ny), ny, nx), nx)
    bx_drain = swap(nx, at.xc, at.at_xc, back_x, got_x, bx_send, bx_recv, right_factor)
    by_block = dot_tn(pick, rows_of(got_x, nx).astype(BF16))
    for m in range(2):
        first = by_block[2 * m * cb : (2 * m + 1) * cb]
        other = by_block[(2 * m + 1) * cb : (2 * m + 2) * cb]
        out[at.z, m] = jnp.where(first_band, first, other).astype(BF16)
    spread(at, TREE, out, last_send, last_recv)

    z_drain()
    x_drain()
    y_drain()
    by_drain()
    bx_drain()
    for store in stores:
        store.wait()


def dma(*shape):
    return pltpu.SemaphoreType.DMA(shape)


HBM_SPEC = pl.BlockSpec(memory_space=pltpu.HBM)
VMEM_SPEC = pl.BlockSpec(memory_space=pltpu.VMEM)


def step(sizes, owner, slot, x, fl, fr, moment, second, bl, br):
    nz, ny, nx = sizes
    width = x.shape[-1]
    arrays = (x, fl, fr, moment, second, bl, br)
    shares = pltpu.VMEM((nz, 2, ny * nx // 4, width), BF16)
    by_x = pltpu.VMEM((nx, ny, width), BF16)
    by_y = pltpu.VMEM((ny, nx, width), BF16)
    news = (fl, fr, moment, second)
    flops = 14 * width**3
    return pl.pallas_call(
        functools.partial(step_kernel, sizes),
        out_shape=(jax.ShapeDtypeStruct((nz, 2, x.shape[2], width), BF16),)
        + tuple(jax.ShapeDtypeStruct(array.shape, array.dtype) for array in news),
        in_specs=[VMEM_SPEC] * 2 + [HBM_SPEC] * 7,
        out_specs=[VMEM_SPEC] + [HBM_SPEC] * 4,
        scratch_shapes=[pltpu.VMEM(array.shape, array.dtype) for array in arrays]
        + [shares] * 3
        + [pltpu.VMEM(array.shape, array.dtype) for array in news]
        + [by_x, by_x, by_y, by_y] * 2
        + [dma(nz, 2)] * 6
        + [dma(nx), dma(nx), dma(ny), dma(ny)] * 2
        + [dma(7), dma(4)],
        compiler_params=pltpu.CompilerParams(
            collective_id=0, has_side_effects=True, vmem_limit_bytes=VMEM_LIMIT
        ),
        cost_estimate=pl.CostEstimate(
            flops=flops, bytes_accessed=9 << 20, transcendentals=width * width
        ),
    )(owner, slot, *arrays)


def shards(sizes, partials, block_owner, owner_slot, fl, fr, moment, second, bl, br):
    size = bl.shape[-1]
    rows, width = partials.shape[2], partials.shape[3]
    x = partials[0].reshape(2, rows, width // size, size)
    flat = (1, block_owner.shape[0])
    back, *news = step(
        sizes, block_owner.reshape(flat), owner_slot.reshape(flat), x, fl, fr, moment, second, bl, br
    )
    update = jnp.transpose(back, (1, 0, 2, 3)).reshape(2, rows, width)
    return (update, *news)


def solution(mesh):
    nz, shard = mesh.shape["dp"], mesh.shape["shard"]
    nx = 8
    blocks = P("shard", None, None)
    return jax.shard_map(
        functools.partial(shards, (nz, shard // nx, nx)),
        mesh=mesh,
        in_specs=(P("dp", None, "shard", None), P(), P()) + (blocks,) * 6,
        out_specs=(P(None, "shard", None),) + (blocks,) * 4,
        check_vma=False,
    )
```

```python
import functools

import jax
import jax.numpy as jnp
from jax import lax
from jax.experimental import pallas as pl
from jax.experimental.pallas import tpu as pltpu
from jax.sharding import PartitionSpec as P

MESH = pl.DeviceIdType.MESH
F32 = jnp.float32
BF16 = jnp.bfloat16
VMEM_LIMIT = 60 << 20


def dot(a, b):
    return jnp.dot(a, b, preferred_element_type=F32)


def dot_tn(a, b):
    return lax.dot_general(a, b, (((0,), (0,)), ((), ())), preferred_element_type=F32)


def dot_nt(a, b):
    return lax.dot_general(a, b, (((1,), (1,)), ((), ())), preferred_element_type=F32)


class Place:
    def __init__(self, nz, ny, nx):
        self.nz, self.ny, self.nx = nz, ny, nx
        self.z = lax.axis_index("dp")
        self.s = lax.axis_index("shard")
        self.y = self.s // nx
        self.xc = self.s % nx

    def at_z(self, step):
        return ((self.z + self.nz + step) % self.nz, self.s)

    def at_xc(self, xc):
        return (self.z, self.y * self.nx + xc)

    def at_y(self, y):
        return (self.z, y * self.nx + self.xc)

    def slot(self, step):
        return (self.z + 2 * self.nz + step) % self.nz


def enter(at):
    barrier = pltpu.get_barrier_semaphore()

    def signal(peer):
        pl.semaphore_signal(barrier, inc=1, device_id=peer, device_id_type=MESH)

    steps = sorted({abs(child - parent) for parent, child in SUM_TREE + TREE})
    for step in steps:
        signal(at.at_z(step))
        signal(at.at_z(-step))

    def to_xc(step, carry):
        signal(at.at_xc((at.xc + step) % at.nx))
        return carry

    def to_y(step, carry):
        signal(at.at_y((at.y + step) % at.ny))
        return carry

    lax.fori_loop(1, at.nx, to_xc, 0)
    lax.fori_loop(1, at.ny, to_y, 0)
    return lambda: pl.semaphore_wait(barrier, 2 * len(steps) + at.nx - 1 + at.ny - 1)


def remote(src, dst, send_sem, recv_sem, peer):
    return pltpu.make_async_remote_copy(
        src_ref=src,
        dst_ref=dst,
        send_sem=send_sem,
        recv_sem=recv_sem,
        device_id=peer,
        device_id_type=MESH,
    )


def swap(count, mine, peer_of, out_buf, in_buf, send_sem, recv_sem, meanwhile=None):
    def start(step, carry):
        j = (mine + step) % count
        remote(out_buf.at[j], in_buf.at[mine], send_sem.at[j], recv_sem.at[mine], peer_of(j)).start()
        return carry

    def finish(step, carry):
        j = (mine + step) % count
        remote(out_buf.at[j], in_buf.at[j], send_sem.at[j], recv_sem.at[j], peer_of(j)).wait_recv()
        return carry

    def drain(step, carry):
        j = (mine + step) % count
        remote(out_buf.at[j], in_buf.at[j], send_sem.at[j], recv_sem.at[j], peer_of(j)).wait_send()
        return carry

    lax.fori_loop(1, count, start, 0)
    in_buf[mine] = out_buf[mine]
    if meanwhile is not None:
        meanwhile()
    lax.fori_loop(1, count, finish, 0)
    return lambda: lax.fori_loop(1, count, drain, 0)


def rows_of(buf, count):
    return jnp.concatenate([buf[j].astype(F32) for j in range(count)], axis=0)


def put_rows(buf, rows, count):
    height = rows.shape[0] // count
    for j in range(count):
        buf[j] = rows[j * height : (j + 1) * height].astype(BF16)


def turned(rows, outer, inner):
    total = outer * inner
    row = lax.broadcasted_iota(jnp.int32, (total, total), 0)
    col = lax.broadcasted_iota(jnp.int32, (total, total), 1)
    pick = (col == (row % outer) * inner + row // outer).astype(F32).astype(BF16)
    return dot(pick, rows.astype(BF16))


def mirrored(right, left):
    edges = []
    for k in range(max(len(right), len(left))):
        edges += right[k : k + 1] + [(-a, -b) for a, b in left[k : k + 1]]
    return tuple(edges)


REACH = [(0, 6), (0, 3), (0, 1), (3, 2), (3, 4), (6, 5), (6, 7)]
TREE = mirrored(REACH + [(6, 8)], REACH)
CHAIN = [(0, 3), (0, 1), (3, 6), (1, 2), (3, 4), (6, 7), (4, 5)]
SUM_TREE = mirrored(CHAIN + [(7, 8)], CHAIN)


def children(tree, node):
    return [child for parent, child in tree if parent == node]


def spread(at, tree, buf, send_sem, recv_sem, meanwhile=None):
    parts = buf.shape[1]

    def edge(parent, child, origin, part):
        ref = buf.at[origin, part]
        sems = send_sem.at[child % at.nz, part], recv_sem.at[child % at.nz, part]
        return remote(ref, ref, *sems, at.at_z(child - parent))

    for part in range(parts):
        for child in children(tree, 0):
            edge(0, child, at.z, part).start()
    if meanwhile is not None:
        meanwhile()
    for parent, node in tree:
        for part in range(parts):
            edge(parent, node, at.slot(-node), part).wait_recv()
            for child in children(tree, node):
                edge(node, child, at.slot(-node), part).start()
    for parent, child in tree:
        for part in range(parts):
            edge(parent, child, at.slot(-parent), part).wait_send()


def collect(at, tree, x, sums, in_buf, send_sem, recv_sem, prepare):
    parts = x.shape[0]

    def edge(parent, child, part):
        inner = children(tree, child)
        src = sums.at[child % at.nz, part] if inner else x.at[part, at.slot(-child)]
        sems = send_sem.at[child % at.nz, part], recv_sem.at[child % at.nz, part]
        return remote(src, in_buf.at[child % at.nz, part], *sems, at.at_z(parent - child))

    def total(node, part):
        value = x[part, at.slot(-node)].astype(F32)
        for child in children(tree, node):
            edge(node, child, part).wait_recv()
            value += in_buf[child % at.nz, part].astype(F32)
        return value

    for part in range(parts):
        prepare(part)
        for parent, child in tree[::-1]:
            if not children(tree, child):
                edge(parent, child, part).start()
    for parent, child in tree[::-1]:
        if children(tree, child):
            for part in range(parts):
                sums[child % at.nz, part] = total(child, part).astype(BF16)
                edge(parent, child, part).start()

    def drain():
        for parent, child in tree:
            for part in range(parts):
                edge(parent, child, part).wait_send()

    return [total(0, part) for part in range(parts)], drain


def to_owners(at, owner, slot, per_owner):
    count = owner.shape[1]
    shape = (at.nx * at.ny, count)
    row = lax.broadcasted_iota(jnp.int32, shape, 0)
    place = (row % at.ny) * at.nx + row // at.ny
    position = owner[...] * per_owner + slot[...]
    return (place == jnp.broadcast_to(position, shape)).astype(F32).astype(BF16)


def step_kernel(sizes, owner, slot, x_in, *refs):
    fl_in, fr_in, moment_in, second_in, bl_in, br_in = refs[:6]
    out, fl_out, fr_out, moment_out, second_out = refs[6:11]
    flat, fl, fr, moment, second, bl, br = loaded = refs[11:18]
    x, sums, in_sums, held, fl_new, fr_new, moment_new, second_new, left_by_z, moment_by_z = refs[18:28]
    out_x, in_x, out_y, in_y, back_x, got_x, back_y, got_y = refs[28:36]
    rs_send, rs_recv, ag_send, ag_recv, last_send, last_recv = refs[36:42]
    x_send, x_recv, y_send, y_recv, bx_send, bx_recv, by_send, by_recv = refs[42:50]
    load_sem, store_sem = refs[50:]
    at = Place(*sizes)
    nz, ny, nx = sizes
    size = bl.shape[-1]
    per_z = size // nz
    half = ny // 2
    cb = out.shape[2]

    stored = (x_in, fl_in, fr_in, moment_in, second_in, bl_in, br_in)
    loads = [
        pltpu.make_async_copy(src, dst, load_sem.at[i])
        for i, (src, dst) in enumerate(zip(stored, loaded))
    ]
    for load in loads:
        load.start()
    entered = enter(at)
    loads[0].wait()

    def prepare(m):
        columns = [flat[m, :, c * size : (c + 1) * size] for c in range(cb)]
        x[m] = turned(jnp.concatenate(columns, axis=0), cb, nz).astype(BF16).reshape(x.shape[1:])
        if m == 0:
            entered()

    total, z_drain = collect(at, SUM_TREE, x, sums, in_sums, rs_send, rs_recv, prepare)

    first_band = at.y < half
    pick = to_owners(at, owner, slot, fl.shape[0])
    none = jnp.zeros_like(total[0])
    placed = []
    for m in range(2):
        placed += [jnp.where(first_band, total[m], none), jnp.where(first_band, none, total[m])]
    put_rows(out_x, dot(pick, jnp.concatenate(placed, axis=0).astype(BF16)), nx)
    x_drain = swap(nx, at.xc, at.at_xc, out_x, in_x, x_send, x_recv)
    put_rows(out_y, turned(rows_of(in_x, nx), nx, ny), ny)
    y_drain = swap(ny, at.y, at.at_y, out_y, in_y, y_send, y_recv)
    mine = [in_y[q].astype(F32) + in_y[q + half].astype(F32) for q in range(half)]
    put_rows(held.at[at.z], jnp.concatenate(mine, axis=0), 2)
    row = lax.broadcasted_iota(jnp.int32, (size, size), 0)
    col = lax.broadcasted_iota(jnp.int32, (size, size), 1)
    order = (col == (row % nz) * per_z + row // nz).astype(F32).astype(BF16)
    own = lax.broadcasted_iota(jnp.int32, (per_z, size), 0) * nz + at.z
    rows = (lax.broadcasted_iota(jnp.int32, (per_z, size), 1) == own).astype(F32).astype(BF16)

    def by_z():
        for load in loads[1:]:
            load.wait()
        left_by_z[...] = dot_tn(order, bl[0]).astype(BF16)
        moment_by_z[...] = dot_tn(order, moment[0]).astype(BF16)

    spread(at, TREE, held, ag_send, ag_recv, by_z)

    g = held[...].reshape(size, size)
    right = br[0]
    rotated = dot(dot_tn(left_by_z[...], g).astype(BF16), right)
    second_next = 0.95 * second[0] + 0.05 * rotated * rotated
    second_new[0] = second_next
    moment_next = (0.9 * moment_by_z[...].astype(F32) + 0.1 * g.astype(F32)).astype(BF16)
    moment_rotated = dot(dot_tn(left_by_z[...], moment_next).astype(BF16), right)
    scaled = (moment_rotated / (jnp.sqrt(second_next) + 1e-8)).astype(BF16)
    back = dot(dot(rows, bl[0]).astype(BF16), scaled).astype(BF16)
    update_rows = dot_nt(back, right)

    stores = [
        pltpu.make_async_copy(src, dst, store_sem.at[i])
        for i, (src, dst) in enumerate(
            (
                (second_new, second_out),
                (moment_new, moment_out),
                (fl_new, fl_out),
                (fr_new, fr_out),
            )
        )
    ]

    def left_factor():
        stores[0].start()
        moment_new[0] = dot(order, moment_next).astype(BF16)
        stores[1].start()
        ordered = dot(order, g).astype(BF16)
        fl_new[0] = 0.95 * fl[0] + 0.05 * dot_nt(ordered, ordered)
        stores[2].start()

    def right_factor():
        fr_new[0] = 0.95 * fr[0] + 0.05 * dot_tn(g, g)
        stores[3].start()

    put_rows(back_y, jnp.concatenate([update_rows, update_rows], axis=0), ny)
    by_drain = swap(ny, at.y, at.at_y, back_y, got_y, by_send, by_recv, left_factor)
    put_rows(back_x, turned(rows_of(got_y, ny), ny, nx), nx)
    bx_drain = swap(nx, at.xc, at.at_xc, back_x, got_x, bx_send, bx_recv, right_factor)
    by_block = dot_tn(pick, rows_of(got_x, nx).astype(BF16))
    for m in range(2):
        first = by_block[2 * m * cb : (2 * m + 1) * cb]
        other = by_block[(2 * m + 1) * cb : (2 * m + 2) * cb]
        out[at.z, m] = jnp.where(first_band, first, other).astype(BF16)
    spread(at, TREE, out, last_send, last_recv)

    z_drain()
    x_drain()
    y_drain()
    by_drain()
    bx_drain()
    for store in stores:
        store.wait()


def dma(*shape):
    return pltpu.SemaphoreType.DMA(shape)


HBM_SPEC = pl.BlockSpec(memory_space=pltpu.HBM)
VMEM_SPEC = pl.BlockSpec(memory_space=pltpu.VMEM)


def step(sizes, owner, slot, x, fl, fr, moment, second, bl, br):
    nz, ny, nx = sizes
    width = bl.shape[-1]
    columns = x.shape[2] // width
    arrays = (x, fl, fr, moment, second, bl, br)
    shares = pltpu.VMEM((nz, 2, ny * nx // 4, width), BF16)
    by_x = pltpu.VMEM((nx, ny, width), BF16)
    by_y = pltpu.VMEM((ny, nx, width), BF16)
    news = (fl, fr, moment, second)
    flops = 14 * width**3
    return pl.pallas_call(
        functools.partial(step_kernel, sizes),
        out_shape=(jax.ShapeDtypeStruct((nz, 2, columns, width), BF16),)
        + tuple(jax.ShapeDtypeStruct(array.shape, array.dtype) for array in news),
        in_specs=[VMEM_SPEC] * 2 + [HBM_SPEC] * 7,
        out_specs=[VMEM_SPEC] + [HBM_SPEC] * 4,
        scratch_shapes=[pltpu.VMEM(array.shape, array.dtype) for array in arrays]
        + [pltpu.VMEM((2, nz, columns, width), BF16)]
        + [shares] * 3
        + [pltpu.VMEM(array.shape, array.dtype) for array in news]
        + [pltpu.VMEM((width, width), BF16)] * 2
        + [by_x, by_x, by_y, by_y] * 2
        + [dma(nz, 2)] * 6
        + [dma(nx), dma(nx), dma(ny), dma(ny)] * 2
        + [dma(7), dma(4)],
        compiler_params=pltpu.CompilerParams(
            collective_id=0, has_side_effects=True, vmem_limit_bytes=VMEM_LIMIT
        ),
        cost_estimate=pl.CostEstimate(
            flops=flops, bytes_accessed=9 << 20, transcendentals=width * width
        ),
    )(owner, slot, *arrays)


def finish_kernel(*refs):
    stored, outs, here, (update, load_sem, store_sem) = refs[:5], refs[5:10], refs[10:15], refs[15:]
    back = here[0]
    loads = [
        pltpu.make_async_copy(src, dst, load_sem.at[i])
        for i, (src, dst) in enumerate(zip(stored, here))
    ]
    stores = [
        pltpu.make_async_copy(src, dst, store_sem.at[i])
        for i, (src, dst) in enumerate(zip((update,) + here[1:], outs))
    ]
    for load in loads:
        load.start()
    nz, _, cb, size = back.shape
    loads[0].wait()
    for m in range(2):
        by_z = jnp.concatenate([back[z, m] for z in range(nz)], axis=0)
        by_column = turned(by_z, nz, cb).astype(BF16)
        for c in range(cb):
            update[m, :, c * size : (c + 1) * size] = by_column[c * nz : (c + 1) * nz]
    stores[0].start()
    for load, store in zip(loads[1:], stores[1:]):
        load.wait()
        store.start()
    for store in stores:
        store.wait()


def finish(back, *news):
    nz, _, cb, size = back.shape
    update = jax.ShapeDtypeStruct((2, nz, cb * size), BF16)
    arrays = (back,) + news
    return pl.pallas_call(
        finish_kernel,
        out_shape=(update,) + tuple(jax.ShapeDtypeStruct(a.shape, a.dtype) for a in news),
        in_specs=[HBM_SPEC] * 5,
        out_specs=[HBM_SPEC] * 5,
        scratch_shapes=[pltpu.VMEM(a.shape, a.dtype) for a in arrays]
        + [pltpu.VMEM(update.shape, BF16), dma(5), dma(5)],
        compiler_params=pltpu.CompilerParams(vmem_limit_bytes=VMEM_LIMIT),
    )(*arrays)


def shards(sizes, partials, block_owner, owner_slot, fl, fr, moment, second, bl, br):
    flat = (1, block_owner.shape[0])
    owner, slot = block_owner.reshape(flat), owner_slot.reshape(flat)
    return finish(*step(sizes, owner, slot, partials[0], fl, fr, moment, second, bl, br))


def solution(mesh):
    nz, shard = mesh.shape["dp"], mesh.shape["shard"]
    nx = 8
    blocks = P("shard", None, None)
    return jax.shard_map(
        functools.partial(shards, (nz, shard // nx, nx)),
        mesh=mesh,
        in_specs=(P("dp", None, "shard", None), P(), P()) + (blocks,) * 6,
        out_specs=(P(None, "shard", None),) + (blocks,) * 4,
        check_vma=False,
    )
```
